128 devices in a mesh: row: 16 (over x, z_lo, core), col: 8 (over y, z_hi).
Axes of the slice: x: 4, y: 4, z: 4 (z_hi: 2, z_lo: 2; z = z_hi * 2 + z_lo), core: 2. Of those that a mesh axis runs over, the one named last changes fastest.
Arguments:
- entities: bfloat16 [2, 131072, 200], P(None, ('row', 'col')), may hold values from -2.390625 to 2.390625
- relations: bfloat16 [2, 1024, 200], replicated, may hold values from -6 to 6
- src_index: int32 [524288], P(('row', 'col')), may hold values from 0 to 8191
- dst_index: int32 [524288], P(('row', 'col')), may hold values from 0 to 16383
- rel_index: int32 [524288], P(('row', 'col')), may hold values from 0 to 1023
- neg_block: int32 [1024], P(('row', 'col')), may hold values from 0 to 31
Outputs:
- edge_loss: float32 [524288], P(('row', 'col'))
- relation_grad: float32 [2, 1024, 200], P(None, ('row', 'col'))
The draws below stay inside these ranges and needn't reach their ends.
All inputs are finite; a program needn't handle non-finite values.
Results may differ from the reference program's by a relative error of at most 0.0018.
Values may be sent and summed in bfloat16 or wider, within the bound.
No kernel may reach another device: no remote copies, remote signals or barrier semaphores. Data moves between devices by JAX's collectives and lax.ppermute only.
A program may use at most 128 MiB of HBM per device.

```python
import jax
import jax.numpy as jnp
from jax import lax

DIM = 200
NREL = 1024
ENT_DEV = 1024
EDGE_DEV = 4096
GROUP = 512
NEGB = 512
NENT = 131072
EDGES = 524288
N_ROW = 16
N_COL = 8


def place_ends(entries, rng, least, largest):
    longest = entries.shape.index(max(entries.shape))
    spots = []
    for shift in (0, 1):
        where = [jax.random.randint(jax.random.fold_in(rng, axis), (), 0, length) for axis, length in enumerate(entries.shape)]
        where[longest] = (where[longest] + shift) % entries.shape[longest]
        spots.append(tuple(where))
    return entries.at[spots[0]].set(least).at[spots[1]].set(largest)


def block_levels(rng, shape, cuts, low, high):
    loudness, own = 1.0, jax.random.fold_in(rng, 6)
    for dim, parts in cuts:
        steps = jnp.exp(jax.random.uniform(jax.random.fold_in(own, dim), (parts,), jnp.float32, low / len(cuts), high / len(cuts)))
        loudness = loudness * jnp.repeat(steps, shape[dim] // parts).reshape([-1 if axis == dim else 1 for axis in range(len(shape))])
    return loudness


def centred(stream_key, extent, width, bound, pieces=(), kind=jnp.bfloat16):
    level = block_levels(stream_key, extent, pieces, -0.22, 0.18) if pieces else 1.0
    array = jax.random.normal(stream_key, extent, jnp.float32) * width * level
    return jnp.minimum(jnp.maximum(array, -bound), bound).astype(kind)


def setup_inputs(seed: int = 0) -> dict:
    key_of = jax.random.split(jax.random.key(seed), 7)
    return {
        "entities": centred(key_of[0], (2, NENT, DIM), 0.4, 2.390625, ((1, 128),)),
        "relations": centred(key_of[1], (2, NREL, DIM), 1.0, 6.0),
        "src_index": place_ends(jax.random.randint(key_of[2], (EDGES,), 0, N_COL * ENT_DEV), jax.random.fold_in(key_of[2], 1), 0, (N_COL * ENT_DEV) - 1).astype(jnp.int32),
        "dst_index": place_ends(jax.random.randint(key_of[3], (EDGES,), 0, N_ROW * ENT_DEV), jax.random.fold_in(key_of[3], 1), 0, (N_ROW * ENT_DEV) - 1).astype(jnp.int32),
        "rel_index": place_ends(jax.random.randint(key_of[4], (EDGES,), 0, NREL), jax.random.fold_in(key_of[4], 1), 0, NREL - 1).astype(jnp.int32),
        "neg_block": place_ends(jax.random.randint(key_of[5], (EDGES // GROUP,), 0, N_ROW * ENT_DEV // NEGB), jax.random.fold_in(key_of[5], 1), 0, (N_ROW * ENT_DEV // NEGB) - 1).astype(jnp.int32),
    }


def bucket_terms(picked_src, picked_dst, negatives, relations, rel_ids):
    onehot = (rel_ids[:, None] == jnp.arange(relations.shape[1], dtype=jnp.int32)[None, :]).astype(jnp.bfloat16)
    rel_re = jnp.dot(onehot, relations[0], preferred_element_type=jnp.float32)
    rel_im = jnp.dot(onehot, relations[1], preferred_element_type=jnp.float32)
    src_re = picked_src[0].astype(jnp.float32)
    src_im = picked_src[1].astype(jnp.float32)
    dst_re = picked_dst[0].astype(jnp.float32)
    dst_im = picked_dst[1].astype(jnp.float32)
    query_re = src_re * rel_re - src_im * rel_im
    query_im = src_re * rel_im + src_im * rel_re
    pos_score = jnp.sum(query_re * dst_re, 1) + jnp.sum(query_im * dst_im, 1)
    groups = negatives.shape[1]
    dim = query_re.shape[1]
    qre_f = query_re.astype(jnp.bfloat16).astype(jnp.float32).reshape(groups, -1, dim)
    qim_f = query_im.astype(jnp.bfloat16).astype(jnp.float32).reshape(groups, -1, dim)
    neg_re = negatives[0].astype(jnp.float32)
    neg_im = negatives[1].astype(jnp.float32)
    neg_score = jnp.einsum("kcd,knd->kcn", qre_f, neg_re, precision=lax.Precision.HIGHEST) + jnp.einsum("kcd,knd->kcn", qim_f, neg_im, precision=lax.Precision.HIGHEST)
    edge_loss = jax.nn.softplus(-pos_score) + jnp.mean(jax.nn.softplus(neg_score), -1).reshape(-1)
    weights = (jax.nn.sigmoid(neg_score) / NEGB).astype(jnp.bfloat16).astype(jnp.float32)
    gneg_re = jnp.einsum("kcn,knd->kcd", weights, neg_re, precision=lax.Precision.HIGHEST).reshape(-1, dim)
    gneg_im = jnp.einsum("kcn,knd->kcd", weights, neg_im, precision=lax.Precision.HIGHEST).reshape(-1, dim)
    pull = jax.nn.sigmoid(-pos_score)[:, None]
    grad_re = gneg_re - pull * dst_re
    grad_im = gneg_im - pull * dst_im
    term_re = (grad_re * src_re + grad_im * src_im).astype(jnp.bfloat16)
    term_im = (grad_im * src_re - grad_re * src_im).astype(jnp.bfloat16)
    dims = (((0,), (0,)), ((), ()))
    rel_grad = jnp.stack([lax.dot_general(onehot, term_re, dims, preferred_element_type=jnp.float32), lax.dot_general(onehot, term_im, dims, preferred_element_type=jnp.float32)], 0)
    return edge_loss, rel_grad


def reference(entities, relations, src_index, dst_index, rel_index, neg_block):
    dim = entities.shape[2]
    grid_rows = entities.reshape(2, N_ROW, N_COL, ENT_DEV, dim)
    groups = EDGE_DEV // GROUP

    def visit(accum, device):
        row_pos = device // N_COL
        col_pos = device % N_COL
        source_rows = lax.dynamic_index_in_dim(grid_rows, row_pos, 1, keepdims=False).reshape(2, N_COL * ENT_DEV, dim)
        target_rows = lax.dynamic_index_in_dim(grid_rows, col_pos, 2, keepdims=False).reshape(2, N_ROW * ENT_DEV, dim)
        sources = lax.dynamic_slice_in_dim(src_index, (device * EDGE_DEV).astype(jnp.int32), EDGE_DEV)
        targets = lax.dynamic_slice_in_dim(dst_index, (device * EDGE_DEV).astype(jnp.int32), EDGE_DEV)
        rel_ids = lax.dynamic_slice_in_dim(rel_index, (device * EDGE_DEV).astype(jnp.int32), EDGE_DEV)
        block_ids = lax.dynamic_slice_in_dim(neg_block, (device * groups).astype(jnp.int32), groups)
        picked_src = jnp.take(source_rows, sources, axis=1)
        picked_dst = jnp.take(target_rows, targets, axis=1)
        negatives = jnp.take(target_rows.reshape(2, -1, NEGB, dim), block_ids, axis=1)
        edge_loss, rel_grad = bucket_terms(picked_src, picked_dst, negatives, relations, rel_ids)
        return accum + rel_grad, edge_loss

    rel_total, losses = lax.scan(visit, jnp.zeros((2, NREL, dim), jnp.float32), jnp.arange(N_ROW * N_COL, dtype=jnp.int32))
    return losses.reshape(-1), rel_total
```

```python
import functools

import jax
import jax.numpy as jnp
from jax import lax
from jax.experimental import pallas as pl
from jax.experimental.pallas import tpu as pltpu
from jax.sharding import PartitionSpec as P

F32, BF16 = jnp.float32, jnp.bfloat16
SHARD = 1024
EDGES = 4096
GROUP = 512
NEGB = 512
HALF = 256
WIDE = 2 * HALF
DIM = 200
NREL = 1024
STEPS = EDGES // GROUP
BOTH = ("row", "col")


def hop(array, dy=0, flip=0):
    pairs = []
    for r in range(16):
        for c in range(8):
            y, h = c // 2, c % 2
            pairs.append((r * 8 + c, r * 8 + ((y + dy) % 4) * 2 + (h ^ flip)))
    return lax.ppermute(array, BOTH, pairs)


def column_shards(own):
    pair = hop(own, flip=1)
    up, down = hop(own, dy=1), hop(own, dy=-1)
    pair_up, pair_down = hop(pair, dy=1), hop(pair, dy=-1)
    up2, pair_down2 = hop(up, dy=1), hop(pair_down, dy=-1)
    c = lax.axis_index("col")
    y, h = c // 2, c % 2
    at = lambda dy, flip: ((y - dy) % 4) * 2 + (h ^ flip)
    order = jnp.stack([at(0, 0), at(0, 1), at(1, 0), at(-1, 0), at(1, 1), at(-1, 1), at(2, 0), at(-2, 1)])
    return [own, pair, up, down, pair_up, pair_down, up2, pair_down2], order.astype(jnp.int32)


def fill_rows(columns, start, table):
    def tile(t, carry):
        n = pl.multiple_of(t * 128, 128)
        for part in range(2):
            head = columns[part, 0:128, pl.ds(n, 128)].astype(F32)
            tail = columns[part, 128:DIM, pl.ds(n, 128)].astype(F32)
            tail = jnp.concatenate([tail, jnp.zeros((HALF - DIM, 128), F32)], 0)
            table[pl.ds(start + n, 128), 2 * part, :] = head.T
            table[pl.ds(start + n, 128), 2 * part + 1, :] = tail.T
        return carry

    lax.fori_loop(0, SHARD // 128, tile, 0)


def pick_rows(index, first, table, rows, unroll=16):
    def step(i, carry):
        b = i * unroll
        values = [table[index[first + b + u]] for u in range(unroll)]
        for u in range(unroll):
            rows[b + u] = values[u]
        return carry

    lax.fori_loop(0, GROUP // unroll, step, 0)


def gather_kernel(count, index, order, *refs):
    shards, out = refs[:count], refs[count]
    held, table, rows, sem = refs[count + 1 :]
    g = pl.program_id(0)

    @pl.when(g == 0)
    def _():
        copies = [pltpu.make_async_copy(shards[j], held.at[j], sem.at[j]) for j in range(count)]
        for copy in copies:
            copy.start()
        for j in range(count):
            copies[j].wait()
            fill_rows(held.at[j], pl.multiple_of(order[j] * SHARD, SHARD), table)

    pick_rows(index, g * GROUP, table, rows)
    for k in range(4):
        out[:, k * 128 : (k + 1) * 128] = rows[:, k, :].astype(BF16)


def gather_rows(shards, order, index):
    count = len(shards)
    return pl.pallas_call(
        functools.partial(gather_kernel, count),
        out_shape=jax.ShapeDtypeStruct((EDGES, WIDE), BF16),
        grid_spec=pltpu.PrefetchScalarGridSpec(
            num_scalar_prefetch=2,
            grid=(STEPS,),
            in_specs=[pl.BlockSpec(memory_space=pl.ANY)] * count,
            out_specs=pl.BlockSpec((GROUP, WIDE), lambda g, *_: (g, 0)),
            scratch_shapes=[
                pltpu.VMEM((count, 2, DIM, SHARD), BF16),
                pltpu.VMEM((count * SHARD, 4, 128), F32),
                pltpu.VMEM((GROUP, 4, 128), F32),
                pltpu.SemaphoreType.DMA((count,)),
            ],
        ),
        compiler_params=pltpu.CompilerParams(vmem_limit_bytes=(8 + 4 * count) << 20),
        cost_estimate=pl.CostEstimate(flops=0, bytes_accessed=(5 + 2 * count) * 4_000_000, transcendentals=0),
        name="gather_rows",
    )(index, order, *shards)


BLOCK = 128


def group_kernel(index, blocks, target, src, rel, rel_ids, loss, grad, held, table, rows, negs, terms, sem):
    g = pl.program_id(0)

    @pl.when(g == 0)
    def _():
        copies = [pltpu.make_async_copy(target.at[j], held.at[j], sem.at[j]) for j in range(16)]
        for copy in copies:
            copy.start()
        negs[...] = jnp.zeros_like(negs)
        grad[...] = jnp.zeros_like(grad)
        for j in range(16):
            copies[j].wait()
            fill_rows(held.at[j], j * SHARD, table)

    pick_rows(index, g * GROUP, table, rows)
    block = blocks[g]
    half = pl.multiple_of((block % 2) * NEGB, NEGB)
    for part in range(2):
        negs[part * HALF : part * HALF + DIM, :] = held[block // 2, part, :, pl.ds(half, NEGB)]

    def piece(i, carry):
        at = pl.ds(pl.multiple_of(i * BLOCK, BLOCK), BLOCK)
        s = [src[at, k * 128 : (k + 1) * 128].astype(F32) for k in range(4)]
        w = [rel[at, k * 128 : (k + 1) * 128].astype(F32) for k in range(4)]
        o = [rows[at, k, :] for k in range(4)]
        q = [s[0] * w[0] - s[2] * w[2], s[1] * w[1] - s[3] * w[3], s[0] * w[2] + s[2] * w[0], s[1] * w[3] + s[3] * w[1]]
        pos = jnp.sum((q[0] * o[0] + q[1] * o[1]) + (q[2] * o[2] + q[3] * o[3]), axis=1, keepdims=True)
        qb = jnp.concatenate([v.astype(BF16) for v in q], axis=1)
        score = lax.dot_general(qb, negs[...], (((1,), (0,)), ((), ())), preferred_element_type=F32)
        low = jnp.exp(-jnp.abs(score))
        up = 1.0 + low
        weight = (jnp.where(score >= 0, 1.0 / NEGB, low * (1.0 / NEGB)) / up).astype(BF16)
        peak = jnp.maximum(score, 0.0)
        excess, total = low[:, 0:128], peak[:, 0:128]
        for k in range(1, 4):
            cut = slice(k * 128, (k + 1) * 128)
            excess = excess * up[:, cut] + low[:, cut]
            total = total + peak[:, cut]
        pull_low = jnp.exp(-jnp.abs(pos))
        pull = jnp.where(pos >= 0, pull_low, 1.0) / (1.0 + pull_low)
        pos_loss = jnp.maximum(-pos, 0.0) + jnp.log1p(pull_low)
        loss_part = (total + jnp.log1p(excess)) * (1.0 / NEGB) + pos_loss * (1.0 / 128)
        loss[0, :, at] = lax.dot_general(
            jnp.ones((8, 128), F32), loss_part, (((1,), (1,)), ((), ())),
            precision=lax.Precision.HIGHEST, preferred_element_type=F32,
        )[0:1]
        gneg = lax.dot_general(weight, negs[...], (((1,), (1,)), ((), ())), preferred_element_type=F32)
        d = [gneg[:, k * 128 : (k + 1) * 128] - pull * o[k] for k in range(4)]
        term = [d[0] * s[0] + d[2] * s[2], d[1] * s[1] + d[3] * s[3], d[2] * s[0] - d[0] * s[2], d[3] * s[1] - d[1] * s[3]]
        for k in range(4):
            terms[at, k * 128 : (k + 1) * 128] = term[k].astype(BF16)
        return carry

    for i in range(GROUP // BLOCK):
        piece(i, 0)
    ids = rel_ids[0]

    def scatter(i, carry):
        at = pl.ds(pl.multiple_of(i * 256, 256), 256)
        hot = (lax.broadcasted_iota(jnp.int32, (256, GROUP), 0) + i * 256) == ids
        hot = jnp.where(hot, 1.0, 0.0).astype(BF16)
        grad[at, :] += jnp.dot(hot, terms[...], preferred_element_type=F32)
        return carry

    lax.fori_loop(0, NREL // 256, scatter, 0)


def score_groups(target, dst_index, neg_block, src, rel, rel_index):
    return pl.pallas_call(
        group_kernel,
        out_shape=(jax.ShapeDtypeStruct((STEPS, 1, GROUP), F32), jax.ShapeDtypeStruct((NREL, WIDE), F32)),
        grid_spec=pltpu.PrefetchScalarGridSpec(
            num_scalar_prefetch=2,
            grid=(STEPS,),
            in_specs=[
                pl.BlockSpec(memory_space=pl.ANY),
                pl.BlockSpec((GROUP, WIDE), lambda g, *_: (g, 0)),
                pl.BlockSpec((GROUP, WIDE), lambda g, *_: (g, 0)),
                pl.BlockSpec((1, 1, GROUP), lambda g, *_: (g, 0, 0)),
            ],
            out_specs=[
                pl.BlockSpec((1, 1, GROUP), lambda g, *_: (g, 0, 0)),
                pl.BlockSpec((NREL, WIDE), lambda g, *_: (0, 0)),
            ],
            scratch_shapes=[
                pltpu.VMEM((16, 2, DIM, SHARD), BF16),
                pltpu.VMEM((16 * SHARD, 4, 128), F32),
                pltpu.VMEM((GROUP, 4, 128), F32),
                pltpu.VMEM((WIDE, NEGB), BF16),
                pltpu.VMEM((GROUP, WIDE), BF16),
                pltpu.SemaphoreType.DMA((16,)),
            ],
        ),
        compiler_params=pltpu.CompilerParams(vmem_limit_bytes=60 << 20),
        cost_estimate=pl.CostEstimate(flops=20_000_000_000, bytes_accessed=24_000_000, transcendentals=4_000_000),
        name="score_groups",
    )(dst_index, neg_block, target, src, rel, rel_index.reshape(STEPS, 1, GROUP))


def body(entities, relations, src_index, dst_index, rel_index, neg_block):
    own = jnp.swapaxes(entities, 1, 2)
    target = lax.all_gather(own, "row", axis=0)
    rel = gather_rows([jnp.swapaxes(relations, 1, 2)], jnp.zeros((1,), jnp.int32), rel_index)
    shards, order = column_shards(own)
    src = gather_rows(shards, order, src_index)
    loss, grad = score_groups(target, dst_index, neg_block, src, rel, rel_index)
    parts = lax.all_to_all(grad.reshape(128, 8, WIDE), BOTH, 0, 0, tiled=True)
    share = jnp.sum(parts, axis=0)
    share = jnp.stack([share[:, :DIM], share[:, HALF : HALF + DIM]])
    return loss.reshape(EDGES), share


def solution(mesh):
    placed = (
        P(None, BOTH, None),
        P(),
        P(BOTH),
        P(BOTH),
        P(BOTH),
        P(BOTH),
    )
    return jax.shard_map(
        body,
        mesh=mesh,
        in_specs=placed,
        out_specs=(P(BOTH), P(None, BOTH, None)),
        check_vma=False,
    )
```

```python
import functools

import jax
import jax.numpy as jnp
from jax import lax
from jax.experimental import pallas as pl
from jax.experimental.pallas import tpu as pltpu
from jax.sharding import PartitionSpec as P

F32, BF16 = jnp.float32, jnp.bfloat16
SHARD = 1024
EDGES = 4096
GROUP = 512
NEGB = 512
HALF = 256
WIDE = 2 * HALF
DIM = 200
NREL = 1024
STEPS = EDGES // GROUP
BOTH = ("row", "col")


def hop(array, dy=0, flip=0):
    pairs = []
    for r in range(16):
        for c in range(8):
            y, h = c // 2, c % 2
            pairs.append((r * 8 + c, r * 8 + ((y + dy) % 4) * 2 + (h ^ flip)))
    return lax.ppermute(array, BOTH, pairs)


def column_shards(own):
    tie = lax.optimization_barrier

    def ring(held):
        near = tie((hop(held, dy=1), hop(held, dy=-1)))
        far = hop(near[0][:1], dy=1), hop(near[1][1:], dy=-1)
        return near, far

    pair = hop(own, flip=1)
    near, far = ring(own)
    pair, *far = tie((pair, *far))
    pair_near, pair_far = ring(pair)
    pieces = [(own, 0, None), (near[0], 1, None), (near[1], 2, None), (far[0], 3, 0), (far[1], 3, 1)]
    pieces += [(pair, 4, None), (pair_near[0], 5, None), (pair_near[1], 6, None), (pair_far[0], 7, 0), (pair_far[1], 7, 1)]
    c = lax.axis_index("col")
    y, h = c // 2, c % 2
    order = jnp.stack([((y + dy) % 4) * 2 + (h ^ flip) for flip in (0, 1) for dy in (0, -1, 1, 2)])
    return pieces, order.astype(jnp.int32)


def fill_rows(columns, start, table):
    def tile(t, carry):
        n = pl.multiple_of(t * 128, 128)
        for part in range(2):
            head = columns[part, 0:128, pl.ds(n, 128)].astype(F32)
            tail = columns[part, 128:DIM, pl.ds(n, 128)].astype(F32)
            tail = jnp.concatenate([tail, jnp.zeros((HALF - DIM, 128), F32)], 0)
            at = part * HALF
            table[pl.ds(start + n, 128), at : at + 128] = head.T
            table[pl.ds(start + n, 128), at + 128 : at + HALF] = tail.T
        return carry

    lax.fori_loop(0, SHARD // 128, tile, 0)


def pick_rows(index, first, table, rows, unroll=16):
    def step(i, carry):
        b = i * unroll
        values = [table[pl.ds(index[first + b + u], 1), :] for u in range(unroll)]
        for u in range(0, unroll, 8):
            rows[pl.ds(pl.multiple_of(b + u, 8), 8), :] = jnp.concatenate(values[u : u + 8], 0)
        return carry

    lax.fori_loop(0, GROUP // unroll, step, 0)


def gather_kernel(places, index, order, *refs):
    count = len(places)
    pieces, out = refs[:count], refs[count]
    held, table, rows, sem = refs[count + 1 :]
    g = pl.program_id(0)

    @pl.when(g == 0)
    def _():
        copies = []
        for piece, (slot, part) in zip(pieces, places):
            into = held.at[slot] if part is None else held.at[slot, pl.ds(part, 1)]
            copies.append(pltpu.make_async_copy(piece, into, sem.at[len(copies)]))
            copies[-1].start()
        for j, (slot, part) in enumerate(places):
            copies[j].wait()
            if part != 0:
                fill_rows(held.at[slot], pl.multiple_of(order[slot] * SHARD, SHARD), table)

    pick_rows(index, g * GROUP, table, rows)
    out[...] = rows[...].astype(BF16)


def gather_rows(pieces, order, index):
    places = tuple((slot, part) for _, slot, part in pieces)
    count = places[-1][0] + 1
    return pl.pallas_call(
        functools.partial(gather_kernel, places),
        out_shape=jax.ShapeDtypeStruct((EDGES, WIDE), BF16),
        grid_spec=pltpu.PrefetchScalarGridSpec(
            num_scalar_prefetch=2,
            grid=(STEPS,),
            in_specs=[pl.BlockSpec(memory_space=pl.ANY)] * len(places),
            out_specs=pl.BlockSpec((GROUP, WIDE), lambda g, *_: (g, 0)),
            scratch_shapes=[
                pltpu.VMEM((count, 2, DIM, SHARD), BF16),
                pltpu.VMEM((count * SHARD, WIDE), F32),
                pltpu.VMEM((GROUP, WIDE), F32),
                pltpu.SemaphoreType.DMA((len(places),)),
            ],
        ),
        compiler_params=pltpu.CompilerParams(vmem_limit_bytes=(8 + 4 * count) << 20),
        cost_estimate=pl.CostEstimate(flops=0, bytes_accessed=(5 + 2 * count) * 4_000_000, transcendentals=0),
        name="gather_rows",
    )(index, order, *[piece for piece, _, _ in pieces])


BLOCK = 256


def group_kernel(index, blocks, target, src, rel, rel_ids, loss, keep, give, held, table, rows, negs, terms, sem):
    g = pl.program_id(0)

    @pl.when(g == 0)
    def _():
        copies = [pltpu.make_async_copy(target.at[j], held.at[j], sem.at[j]) for j in range(16)]
        for copy in copies:
            copy.start()
        negs[...] = jnp.zeros_like(negs)
        keep[...] = jnp.zeros_like(keep)
        give[...] = jnp.zeros_like(give)
        for j in range(16):
            copies[j].wait()
            fill_rows(held.at[j], j * SHARD, table)

    @pl.when(g == 0)
    def _():
        pick_rows(index, 0, table, rows)
    block = blocks[g]
    half = pl.multiple_of((block % 2) * NEGB, NEGB)
    for part in range(2):
        negs[part * HALF : part * HALF + DIM, :] = held[block // 2, part, :, pl.ds(half, NEGB)]

    def piece(i, carry):
        at = pl.ds(pl.multiple_of(i * BLOCK, BLOCK), BLOCK)
        s = [src[at, k * 128 : (k + 1) * 128].astype(F32) for k in range(4)]
        w = [rel[at, k * 128 : (k + 1) * 128].astype(F32) for k in range(4)]
        o = [rows[at, k * 128 : (k + 1) * 128] for k in range(4)]
        q = [s[0] * w[0] - s[2] * w[2], s[1] * w[1] - s[3] * w[3], s[0] * w[2] + s[2] * w[0], s[1] * w[3] + s[3] * w[1]]
        pos = jnp.sum((q[0] * o[0] + q[1] * o[1]) + (q[2] * o[2] + q[3] * o[3]), axis=1, keepdims=True)
        qb = jnp.concatenate([v.astype(BF16) for v in q], axis=1)
        score = lax.dot_general(qb, negs[...], (((1,), (0,)), ((), ())), preferred_element_type=F32)
        low = jnp.exp(-jnp.abs(score))
        up = 1.0 + low
        weight = (jnp.where(score >= 0, 1.0 / NEGB, low * (1.0 / NEGB)) / up).astype(BF16)
        peak = jnp.maximum(score, 0.0)
        excess, total = low[:, 0:128], peak[:, 0:128]
        for k in range(1, 4):
            cut = slice(k * 128, (k + 1) * 128)
            excess = excess * up[:, cut] + low[:, cut]
            total = total + peak[:, cut]
        pull_low = jnp.exp(-jnp.abs(pos))
        pull = jnp.where(pos >= 0, pull_low, 1.0) / (1.0 + pull_low)
        pos_loss = jnp.maximum(-pos, 0.0) + jnp.log1p(pull_low)
        loss_part = (total + jnp.log1p(excess)) * (1.0 / NEGB) + pos_loss * (1.0 / 128)
        loss[0, :, at] = jnp.sum(loss_part.T, axis=0, keepdims=True)
        gneg = lax.dot_general(weight, negs[...], (((1,), (1,)), ((), ())), preferred_element_type=F32)
        d = [gneg[:, k * 128 : (k + 1) * 128] - pull * o[k] for k in range(4)]
        term = [d[0] * s[0] + d[2] * s[2], d[1] * s[1] + d[3] * s[3], d[2] * s[0] - d[0] * s[2], d[3] * s[1] - d[1] * s[3]]
        for k in range(4):
            terms[at, k * 128 : (k + 1) * 128] = term[k].astype(BF16)
        return carry

    nxt = jnp.minimum(g + 1, STEPS - 1) * GROUP
    for i in range(GROUP // BLOCK):
        piece(i, 0)
        for b in range(i * BLOCK, (i + 1) * BLOCK, 8):
            rows[b : b + 8, :] = jnp.concatenate([table[pl.ds(index[nxt + b + u], 1), :] for u in range(8)], 0)
    ids = rel_ids[0]

    hot = lax.broadcasted_iota(jnp.int32, (NREL, GROUP), 0) == ids
    hot = jnp.where(hot, 1.0, 0.0).astype(BF16)
    grad = jnp.dot(hot, terms[...], preferred_element_type=F32)
    keep[...] += grad[: NREL // 2]
    give[...] += grad[NREL // 2 :]


def score_groups(target, dst_index, neg_block, src, rel, places):
    return pl.pallas_call(
        group_kernel,
        out_shape=(
            jax.ShapeDtypeStruct((STEPS, 1, GROUP), F32),
            jax.ShapeDtypeStruct((NREL // 2, WIDE), F32),
            jax.ShapeDtypeStruct((NREL // 2, WIDE), F32),
        ),
        grid_spec=pltpu.PrefetchScalarGridSpec(
            num_scalar_prefetch=2,
            grid=(STEPS,),
            in_specs=[
                pl.BlockSpec(memory_space=pl.ANY),
                pl.BlockSpec((GROUP, WIDE), lambda g, *_: (g, 0)),
                pl.BlockSpec((GROUP, WIDE), lambda g, *_: (g, 0)),
                pl.BlockSpec((1, 1, GROUP), lambda g, *_: (g, 0, 0)),
            ],
            out_specs=[
                pl.BlockSpec((1, 1, GROUP), lambda g, *_: (g, 0, 0)),
                pl.BlockSpec((NREL // 2, WIDE), lambda g, *_: (0, 0)),
                pl.BlockSpec((NREL // 2, WIDE), lambda g, *_: (0, 0)),
            ],
            scratch_shapes=[
                pltpu.VMEM((16, 2, DIM, SHARD), BF16),
                pltpu.VMEM((16 * SHARD, WIDE), F32),
                pltpu.VMEM((GROUP, WIDE), F32),
                pltpu.VMEM((WIDE, NEGB), BF16),
                pltpu.VMEM((GROUP, WIDE), BF16),
                pltpu.SemaphoreType.DMA((16,)),
            ],
        ),
        compiler_params=pltpu.CompilerParams(vmem_limit_bytes=60 << 20),
        cost_estimate=pl.CostEstimate(flops=20_000_000_000, bytes_accessed=24_000_000, transcendentals=4_000_000),
        name="score_groups",
    )(dst_index, neg_block, target, src, rel, places.reshape(STEPS, 1, GROUP))


def sum_at_owner(keep, give):
    half = keep + lax.ppermute(give, BOTH, [(d, d ^ 8) for d in range(128)])
    groups = [[a * 16 + core * 8 + c for a in range(8) for c in range(8)] for core in range(2)]
    parts = lax.all_to_all(half.reshape(64, 8, WIDE), BOTH, 0, 0, axis_index_groups=groups, tiled=True)
    return jnp.sum(parts, axis=0)


def body(entities, relations, src_index, dst_index, rel_index, neg_block):
    own = jnp.swapaxes(entities, 1, 2)
    target = lax.all_gather(own, "row", axis=0)
    rel = gather_rows([(jnp.swapaxes(relations, 1, 2), 0, None)], jnp.zeros((1,), jnp.int32), rel_index)
    pieces, order = column_shards(own)
    src = gather_rows(pieces, order, src_index)
    core = lax.axis_index("row") % 2
    places = (((rel_index >> 6) & 1) ^ core) * 512 + (rel_index >> 7) * 64 + (rel_index & 63)
    loss, keep, give = score_groups(target, dst_index, neg_block, src, rel, places)
    share = sum_at_owner(keep, give)
    share = jnp.stack([share[:, :DIM], share[:, HALF : HALF + DIM]])
    return loss.reshape(EDGES), share


def solution(mesh):
    placed = (
        P(None, BOTH, None),
        P(),
        P(BOTH),
        P(BOTH),
        P(BOTH),
        P(BOTH),
    )
    return jax.shard_map(
        body,
        mesh=mesh,
        in_specs=placed,
        out_specs=(P(BOTH), P(None, BOTH, None)),
        check_vma=False,
    )
```

```python
import functools

import jax
import jax.numpy as jnp
from jax import lax
from jax.experimental import pallas as pl
from jax.experimental.pallas import tpu as pltpu
from jax.sharding import PartitionSpec as P

F32, BF16 = jnp.float32, jnp.bfloat16
SHARD = 1024
EDGES = 4096
GROUP = 512
NEGB = 512
HALF = 256
WIDE = 2 * HALF
DIM = 200
NREL = 1024
STEPS = EDGES // GROUP
BOTH = ("row", "col")


def hop(array, dy=0, flip=0):
    pairs = []
    for r in range(16):
        for c in range(8):
            y, h = c // 2, c % 2
            pairs.append((r * 8 + c, r * 8 + ((y + dy) % 4) * 2 + (h ^ flip)))
    return lax.ppermute(array, BOTH, pairs)


def column_shards(own, first):
    tie = lax.optimization_barrier

    def ring(held):
        near = tie((hop(held, dy=1), hop(held, dy=-1)))
        far = hop(near[0][:1], dy=1), hop(near[1][1:], dy=-1)
        return near, far

    pair = hop(own, flip=1)
    near, far = ring(own)
    pair, first, *far = tie((pair, first, *far))
    pair_near, pair_far = ring(pair)
    pieces = [(own, 0, None), (near[0], 1, None), (near[1], 2, None), (far[0], 3, 0), (far[1], 3, 1)]
    pieces += [(pair, 4, None), (pair_near[0], 5, None), (pair_near[1], 6, None), (pair_far[0], 7, 0), (pair_far[1], 7, 1)]
    c = lax.axis_index("col")
    y, h = c // 2, c % 2
    order = jnp.stack([((y + dy) % 4) * 2 + (h ^ flip) for flip in (0, 1) for dy in (0, -1, 1, 2)])
    return pieces, order.astype(jnp.int32), first


def fill_rows(columns, start, table):
    def tile(t, carry):
        n = pl.multiple_of(t * 128, 128)
        for part in range(2):
            head = columns[part, 0:128, pl.ds(n, 128)].astype(F32)
            tail = columns[part, 128:DIM, pl.ds(n, 128)].astype(F32)
            tail = jnp.concatenate([tail, jnp.zeros((HALF - DIM, 128), F32)], 0)
            at = part * HALF
            table[pl.ds(start + n, 128), at : at + 128] = head.T
            table[pl.ds(start + n, 128), at + 128 : at + HALF] = tail.T
        return carry

    lax.fori_loop(0, SHARD // 128, tile, 0)


def pick_rows(index, first, table, rows, unroll=16):
    def step(i, carry):
        b = i * unroll
        values = [table[pl.ds(index[first + b + u], 1), :] for u in range(unroll)]
        for u in range(0, unroll, 8):
            rows[pl.ds(pl.multiple_of(b + u, 8), 8), :] = jnp.concatenate(values[u : u + 8], 0)
        return carry

    lax.fori_loop(0, GROUP // unroll, step, 0)


def gather_kernel(places, index, order, *refs):
    count = len(places)
    pieces, out = refs[:count], refs[count]
    held, table, rows, sem = refs[count + 1 :]
    g = pl.program_id(0)

    @pl.when(g == 0)
    def _():
        copies = []
        for piece, (slot, part) in zip(pieces, places):
            into = held.at[slot] if part is None else held.at[slot, pl.ds(part, 1)]
            copies.append(pltpu.make_async_copy(piece, into, sem.at[len(copies)]))
            copies[-1].start()
        for j, (slot, part) in enumerate(places):
            copies[j].wait()
            if part != 0:
                fill_rows(held.at[slot], pl.multiple_of(order[slot] * SHARD, SHARD), table)

    pick_rows(index, g * GROUP, table, rows)
    out[...] = rows[...].astype(BF16)


def gather_rows(pieces, order, index):
    places = tuple((slot, part) for _, slot, part in pieces)
    count = places[-1][0] + 1
    return pl.pallas_call(
        functools.partial(gather_kernel, places),
        out_shape=jax.ShapeDtypeStruct((EDGES, WIDE), BF16),
        grid_spec=pltpu.PrefetchScalarGridSpec(
            num_scalar_prefetch=2,
            grid=(STEPS,),
            in_specs=[pl.BlockSpec(memory_space=pl.ANY)] * len(places),
            out_specs=pl.BlockSpec((GROUP, WIDE), lambda g, *_: (g, 0)),
            scratch_shapes=[
                pltpu.VMEM((count, 2, DIM, SHARD), BF16),
                pltpu.VMEM((count * SHARD, WIDE), F32),
                pltpu.VMEM((GROUP, WIDE), F32),
                pltpu.SemaphoreType.DMA((len(places),)),
            ],
        ),
        compiler_params=pltpu.CompilerParams(vmem_limit_bytes=60 << 20),
        cost_estimate=pl.CostEstimate(flops=0, bytes_accessed=(5 + 2 * count) * 4_000_000, transcendentals=0),
        name="gather_rows",
    )(index, order, *[piece for piece, _, _ in pieces])


BLOCK = 256


def group_kernel(index, blocks, target, src, rel, rel_ids, loss, keep, give, held, table, rows, negs, terms, sem):
    g = pl.program_id(0)

    @pl.when(g == 0)
    def _():
        copies = [pltpu.make_async_copy(target.at[j], held.at[j], sem.at[j]) for j in range(16)]
        for copy in copies:
            copy.start()
        negs[...] = jnp.zeros_like(negs)
        keep[...] = jnp.zeros_like(keep)
        give[...] = jnp.zeros_like(give)
        for j in range(16):
            copies[j].wait()
            fill_rows(held.at[j], j * SHARD, table)

    @pl.when(g == 0)
    def _():
        pick_rows(index, 0, table, rows)
    block = blocks[g]
    half = pl.multiple_of((block % 2) * NEGB, NEGB)
    for part in range(2):
        negs[part * HALF : part * HALF + DIM, :] = held[block // 2, part, :, pl.ds(half, NEGB)]

    def piece(i, carry):
        at = pl.ds(pl.multiple_of(i * BLOCK, BLOCK), BLOCK)
        s = [src[at, k * 128 : (k + 1) * 128].astype(F32) for k in range(4)]
        w = [rel[at, k * 128 : (k + 1) * 128].astype(F32) for k in range(4)]
        o = [rows[at, k * 128 : (k + 1) * 128] for k in range(4)]
        q = [s[0] * w[0] - s[2] * w[2], s[1] * w[1] - s[3] * w[3], s[0] * w[2] + s[2] * w[0], s[1] * w[3] + s[3] * w[1]]
        pos = jnp.sum((q[0] * o[0] + q[1] * o[1]) + (q[2] * o[2] + q[3] * o[3]), axis=1, keepdims=True)
        qb = jnp.concatenate([v.astype(BF16) for v in q], axis=1)
        score = lax.dot_general(qb, negs[...], (((1,), (0,)), ((), ())), preferred_element_type=F32)
        low = jnp.exp(-jnp.abs(score))
        up = 1.0 + low
        weight = (jnp.where(score >= 0, 1.0 / NEGB, low * (1.0 / NEGB)) / up).astype(BF16)
        peak = jnp.maximum(score, 0.0)
        excess, total = low[:, 0:128], peak[:, 0:128]
        for k in range(1, 4):
            cut = slice(k * 128, (k + 1) * 128)
            excess = excess * up[:, cut] + low[:, cut]
            total = total + peak[:, cut]
        pull_low = jnp.exp(-jnp.abs(pos))
        pull = jnp.where(pos >= 0, pull_low, 1.0) / (1.0 + pull_low)
        pos_loss = jnp.maximum(-pos, 0.0) + jnp.log1p(pull_low)
        loss_part = (total + jnp.log1p(excess)) * (1.0 / NEGB) + pos_loss * (1.0 / 128)
        loss[0, :, at] = jnp.sum(loss_part.T, axis=0, keepdims=True)
        gneg = lax.dot_general(weight, negs[...], (((1,), (1,)), ((), ())), preferred_element_type=F32)
        d = [gneg[:, k * 128 : (k + 1) * 128] - pull * o[k] for k in range(4)]
        term = [d[0] * s[0] + d[2] * s[2], d[1] * s[1] + d[3] * s[3], d[2] * s[0] - d[0] * s[2], d[3] * s[1] - d[1] * s[3]]
        for k in range(4):
            terms[at, k * 128 : (k + 1) * 128] = term[k].astype(BF16)
        return carry

    nxt = jnp.minimum(g + 1, STEPS - 1) * GROUP
    for i in range(GROUP // BLOCK):
        piece(i, 0)
        for b in range(i * BLOCK, (i + 1) * BLOCK, 8):
            rows[b : b + 8, :] = jnp.concatenate([table[pl.ds(index[nxt + b + u], 1), :] for u in range(8)], 0)
    ids = rel_ids[0]

    hot = lax.broadcasted_iota(jnp.int32, (NREL, GROUP), 0) == ids
    hot = jnp.where(hot, 1.0, 0.0).astype(BF16)
    grad = jnp.dot(hot, terms[...], preferred_element_type=F32)
    keep[...] += grad[: NREL // 2]
    give[...] += grad[NREL // 2 :]


def score_groups(target, dst_index, neg_block, src, rel, places):
    return pl.pallas_call(
        group_kernel,
        out_shape=(
            jax.ShapeDtypeStruct((STEPS, 1, GROUP), F32),
            jax.ShapeDtypeStruct((NREL // 2, WIDE), F32),
            jax.ShapeDtypeStruct((NREL // 2, WIDE), F32),
        ),
        grid_spec=pltpu.PrefetchScalarGridSpec(
            num_scalar_prefetch=2,
            grid=(STEPS,),
            in_specs=[
                pl.BlockSpec(memory_space=pl.ANY),
                pl.BlockSpec((GROUP, WIDE), lambda g, *_: (g, 0)),
                pl.BlockSpec((GROUP, WIDE), lambda g, *_: (g, 0)),
                pl.BlockSpec((1, 1, GROUP), lambda g, *_: (g, 0, 0)),
            ],
            out_specs=[
                pl.BlockSpec((1, 1, GROUP), lambda g, *_: (g, 0, 0)),
                pl.BlockSpec((NREL // 2, WIDE), lambda g, *_: (0, 0)),
                pl.BlockSpec((NREL // 2, WIDE), lambda g, *_: (0, 0)),
            ],
            scratch_shapes=[
                pltpu.VMEM((16, 2, DIM, SHARD), BF16),
                pltpu.VMEM((16 * SHARD, WIDE), F32),
                pltpu.VMEM((GROUP, WIDE), F32),
                pltpu.VMEM((WIDE, NEGB), BF16),
                pltpu.VMEM((GROUP, WIDE), BF16),
                pltpu.SemaphoreType.DMA((16,)),
            ],
        ),
        compiler_params=pltpu.CompilerParams(vmem_limit_bytes=60 << 20),
        cost_estimate=pl.CostEstimate(flops=20_000_000_000, bytes_accessed=24_000_000, transcendentals=4_000_000),
        name="score_groups",
    )(dst_index, neg_block, target, src, rel, places.reshape(STEPS, 1, GROUP))


def sum_at_owner(keep, give):
    half = keep + lax.ppermute(give, BOTH, [(d, d ^ 8) for d in range(128)])
    groups = [[a * 16 + core * 8 + c for a in range(8) for c in range(8)] for core in range(2)]
    parts = lax.all_to_all(half.reshape(64, 8, WIDE), BOTH, 0, 0, axis_index_groups=groups, tiled=True)
    return jnp.sum(parts, axis=0)


def body(entities, relations, src_index, dst_index, rel_index, neg_block):
    own = jnp.swapaxes(entities, 1, 2)
    target = lax.all_gather(own, "row", axis=0)
    rel = gather_rows([(jnp.swapaxes(relations, 1, 2), 0, None)], jnp.zeros((1,), jnp.int32), rel_index)
    pieces, order, rel = column_shards(own, rel)
    src = gather_rows(pieces, order, src_index)
    core = lax.axis_index("row") % 2
    places = (((rel_index >> 6) & 1) ^ core) * 512 + (rel_index >> 7) * 64 + (rel_index & 63)
    loss, keep, give = score_groups(target, dst_index, neg_block, src, rel, places)
    share = sum_at_owner(keep, give)
    share = jnp.stack([share[:, :DIM], share[:, HALF : HALF + DIM]])
    return loss.reshape(EDGES), share


def solution(mesh):
    placed = (
        P(None, BOTH, None),
        P(),
        P(BOTH),
        P(BOTH),
        P(BOTH),
        P(BOTH),
    )
    return jax.shard_map(
        body,
        mesh=mesh,
        in_specs=placed,
        out_specs=(P(BOTH), P(None, BOTH, None)),
        check_vma=False,
    )
```

```python
import functools

import jax
import jax.numpy as jnp
from jax import lax
from jax.experimental import pallas as pl
from jax.experimental.pallas import tpu as pltpu
from jax.sharding import PartitionSpec as P

F32, BF16 = jnp.float32, jnp.bfloat16
SHARD = 1024
EDGES = 4096
GROUP = 512
NEGB = 512
HALF = 256
WIDE = 2 * HALF
DIM = 200
NREL = 1024
STEPS = EDGES // GROUP
BOTH = ("row", "col")


def hop(array, dy=0, flip=0):
    pairs = []
    for r in range(16):
        for c in range(8):
            y, h = c // 2, c % 2
            pairs.append((r * 8 + c, r * 8 + ((y + dy) % 4) * 2 + (h ^ flip)))
    return lax.ppermute(array, BOTH, pairs)


def column_shards(own, first):
    tie = lax.optimization_barrier

    def ring(held, *rest):
        near = tie((hop(held, dy=1), hop(held, dy=-1), *rest))
        far = hop(near[0][:1], dy=1), hop(near[1][1:], dy=-1)
        return near, far

    pair = hop(own, flip=1)
    (*near, first), far = ring(own, first)
    pair, *far = tie((pair, *far))
    pair_near, pair_far = ring(pair)
    pieces = [(own, 0, None), (near[0], 1, None), (near[1], 2, None), (far[0], 3, 0), (far[1], 3, 1)]
    pieces += [(pair, 4, None), (pair_near[0], 5, None), (pair_near[1], 6, None), (pair_far[0], 7, 0), (pair_far[1], 7, 1)]
    c = lax.axis_index("col")
    y, h = c // 2, c % 2
    order = jnp.stack([((y + dy) % 4) * 2 + (h ^ flip) for flip in (0, 1) for dy in (0, -1, 1, 2)])
    return pieces, order.astype(jnp.int32), first


def fill_rows(columns, start, table):
    def tile(t, carry):
        n = pl.multiple_of(t * 128, 128)
        for part in range(2):
            head = columns[part, 0:128, pl.ds(n, 128)]
            tail = columns[part, 128:DIM, pl.ds(n, 128)].astype(F32)
            tail = jnp.concatenate([tail, jnp.zeros((HALF - DIM, 128), F32)], 0).astype(BF16)
            at = part * HALF
            table[pl.ds(start + n, 128), at : at + 128] = head.T.astype(F32)
            table[pl.ds(start + n, 128), at + 128 : at + HALF] = tail.T.astype(F32)
        return carry

    lax.fori_loop(0, SHARD // 128, tile, 0, unroll=8)


def pick_rows(index, first, table, rows, unroll=16):
    def step(i, carry):
        b = i * unroll
        values = [table[pl.ds(index[first + b + u], 1), :] for u in range(unroll)]
        for u in range(0, unroll, 8):
            rows[pl.ds(pl.multiple_of(b + u, 8), 8), :] = jnp.concatenate(values[u : u + 8], 0)
        return carry

    lax.fori_loop(0, GROUP // unroll, step, 0)


def gather_kernel(places, index, order, *refs):
    count = len(places)
    pieces, out = refs[:count], refs[count]
    held, table, rows, sem = refs[count + 1 :]
    g = pl.program_id(0)

    @pl.when(g == 0)
    def _():
        copies = []
        for piece, (slot, part) in zip(pieces, places):
            into = held.at[slot] if part is None else held.at[slot, pl.ds(part, 1)]
            copies.append(pltpu.make_async_copy(piece, into, sem.at[len(copies)]))
            copies[-1].start()
        for j, (slot, part) in enumerate(places):
            copies[j].wait()
            if part != 0:
                fill_rows(held.at[slot], pl.multiple_of(order[slot] * SHARD, SHARD), table)

    pick_rows(index, g * GROUP, table, rows)
    out[...] = rows[...].astype(BF16)


def gather_rows(pieces, order, index):
    places = tuple((slot, part) for _, slot, part in pieces)
    count = places[-1][0] + 1
    return pl.pallas_call(
        functools.partial(gather_kernel, places),
        out_shape=jax.ShapeDtypeStruct((EDGES, WIDE), BF16),
        grid_spec=pltpu.PrefetchScalarGridSpec(
            num_scalar_prefetch=2,
            grid=(STEPS,),
            in_specs=[pl.BlockSpec(memory_space=pl.ANY)] * len(places),
            out_specs=pl.BlockSpec((GROUP, WIDE), lambda g, *_: (g, 0)),
            scratch_shapes=[
                pltpu.VMEM((count, 2, DIM, SHARD), BF16),
                pltpu.VMEM((count * SHARD, WIDE), F32),
                pltpu.VMEM((GROUP, WIDE), F32),
                pltpu.SemaphoreType.DMA((len(places),)),
            ],
        ),
        compiler_params=pltpu.CompilerParams(vmem_limit_bytes=60 << 20),
        cost_estimate=pl.CostEstimate(flops=0, bytes_accessed=(5 + 2 * count) * 4_000_000, transcendentals=0),
        name="gather_rows",
    )(index, order, *[piece for piece, _, _ in pieces])


AHEAD = 3
BLOCK = 256
CHUNK = 16


def group_kernel(index, blocks, target, src, rel, rel_ids, loss, keep, give, held, table, rows, negs, terms, query, wide, pull, losses, sem):
    g = pl.program_id(0)

    @pl.when(g == 0)
    def _():
        copies = [pltpu.make_async_copy(target.at[j], held.at[j], sem.at[j]) for j in range(16)]
        for copy in copies[:AHEAD]:
            copy.start()
        negs[...] = jnp.zeros_like(negs)
        keep[...] = jnp.zeros_like(keep)
        give[...] = jnp.zeros_like(give)
        for j in range(16):
            copies[j].wait()
            if j + AHEAD < 16:
                copies[j + AHEAD].start()
            fill_rows(held.at[j], j * SHARD, table)

    @pl.when(g == 0)
    def _():
        pick_rows(index, 0, table, rows)
    block = blocks[g]
    half = pl.multiple_of((block % 2) * NEGB, NEGB)
    for part in range(2):
        negs[part * HALF : part * HALF + DIM, :] = held[block // 2, part, :, pl.ds(half, NEGB)]

    nxt = jnp.minimum(g + 1, STEPS - 1) * GROUP
    tiles = [slice(k * 128, (k + 1) * 128) for k in range(4)]

    def queries(at):
        s = [src[at, t].astype(F32) for t in tiles]
        w = [rel[at, t].astype(F32) for t in tiles]
        o = [rows[at, t] for t in tiles]
        q = [s[0] * w[0] - s[2] * w[2], s[1] * w[1] - s[3] * w[3], s[0] * w[2] + s[2] * w[0], s[1] * w[3] + s[3] * w[1]]
        pos = jnp.sum((q[0] * o[0] + q[1] * o[1]) + (q[2] * o[2] + q[3] * o[3]), axis=1, keepdims=True)
        for t, v in zip(tiles, q):
            query[at, t] = v.astype(BF16)
        low = jnp.exp(-jnp.abs(pos))
        pull[at, :] = jnp.broadcast_to(jnp.where(pos >= 0, low, 1.0) / (1.0 + low), (CHUNK, 128))
        losses[at, :] = jnp.broadcast_to((jnp.maximum(-pos, 0.0) + jnp.log1p(low)) * (1.0 / 128), (CHUNK, 128))

    def weights(at):
        for k, t in enumerate(tiles):
            score = wide[at, t]
            low = jnp.exp(-jnp.abs(score))
            up = 1.0 + low
            query[at, t] = (jnp.where(score >= 0, 1.0 / NEGB, low * (1.0 / NEGB)) / up).astype(BF16)
            peak = jnp.maximum(score, 0.0)
            excess = excess * up + low if k else low
            total = total + peak if k else peak
        losses[at, :] += (total + jnp.log1p(excess)) * (1.0 / NEGB)

    def gradients(at):
        s = [src[at, t].astype(F32) for t in tiles]
        p = pull[at, :]
        d = [wide[at, t] - p * rows[at, t] for t in tiles]
        term = [d[0] * s[0] + d[2] * s[2], d[1] * s[1] + d[3] * s[3], d[2] * s[0] - d[0] * s[2], d[3] * s[1] - d[1] * s[3]]
        for t, v in zip(tiles, term):
            terms[at, t] = v.astype(BF16)
        for b in range(at.start, at.stop, 8):
            rows[b : b + 8, :] = jnp.concatenate([table[pl.ds(index[nxt + b + u], 1), :] for u in range(8)], 0)

    blocks_of = [slice(b, b + BLOCK) for b in range(0, GROUP, BLOCK)]
    chunks_of = lambda block: [slice(c, c + CHUNK) for c in range(block.start, block.stop, CHUNK)]
    for block in blocks_of:
        for at in chunks_of(block):
            queries(at)
        wide[block, :] = jnp.dot(query[block, :], negs[...], preferred_element_type=F32)
    for block in blocks_of:
        for at in chunks_of(block):
            weights(at)
        wide[block, :] = lax.dot_general(query[block, :], negs[...], (((1,), (1,)), ((), ())), preferred_element_type=F32)
    for block in blocks_of:
        for at in chunks_of(block):
            gradients(at)
    for b in range(0, GROUP, 128):
        loss[0, :, b : b + 128] = jnp.sum(losses[b : b + 128, :].T, axis=0, keepdims=True)
    ids = rel_ids[0]

    hot = lax.broadcasted_iota(jnp.int32, (NREL, GROUP), 0) == ids
    hot = jnp.where(hot, 1.0, 0.0).astype(BF16)
    grad = jnp.dot(hot, terms[...], preferred_element_type=F32)
    keep[...] += grad[: NREL // 2]
    give[...] += grad[NREL // 2 :]


def score_groups(target, dst_index, neg_block, src, rel, places):
    return pl.pallas_call(
        group_kernel,
        out_shape=(
            jax.ShapeDtypeStruct((STEPS, 1, GROUP), F32),
            jax.ShapeDtypeStruct((NREL // 2, WIDE), F32),
            jax.ShapeDtypeStruct((NREL // 2, WIDE), F32),
        ),
        grid_spec=pltpu.PrefetchScalarGridSpec(
            num_scalar_prefetch=2,
            grid=(STEPS,),
            in_specs=[
                pl.BlockSpec(memory_space=pl.ANY),
                pl.BlockSpec((GROUP, WIDE), lambda g, *_: (g, 0)),
                pl.BlockSpec((GROUP, WIDE), lambda g, *_: (g, 0)),
                pl.BlockSpec((1, 1, GROUP), lambda g, *_: (g, 0, 0)),
            ],
            out_specs=[
                pl.BlockSpec((1, 1, GROUP), lambda g, *_: (g, 0, 0)),
                pl.BlockSpec((NREL // 2, WIDE), lambda g, *_: (0, 0)),
                pl.BlockSpec((NREL // 2, WIDE), lambda g, *_: (0, 0)),
            ],
            scratch_shapes=[
                pltpu.VMEM((16, 2, DIM, SHARD), BF16),
                pltpu.VMEM((16 * SHARD, WIDE), F32),
                pltpu.VMEM((GROUP, WIDE), F32),
                pltpu.VMEM((WIDE, NEGB), BF16),
                pltpu.VMEM((GROUP, WIDE), BF16),
                pltpu.VMEM((GROUP, WIDE), BF16),
                pltpu.VMEM((GROUP, WIDE), F32),
                pltpu.VMEM((GROUP, 128), F32),
                pltpu.VMEM((GROUP, 128), F32),
                pltpu.SemaphoreType.DMA((16,)),
            ],
        ),
        compiler_params=pltpu.CompilerParams(vmem_limit_bytes=60 << 20),
        cost_estimate=pl.CostEstimate(flops=20_000_000_000, bytes_accessed=24_000_000, transcendentals=4_000_000),
        name="score_groups",
    )(dst_index, neg_block, target, src, rel, places.reshape(STEPS, 1, GROUP))


def sum_at_owner(keep, give):
    half = keep + lax.ppermute(give, BOTH, [(d, d ^ 8) for d in range(128)])
    groups = [[a * 16 + core * 8 + c for a in range(8) for c in range(8)] for core in range(2)]
    parts = lax.all_to_all(half.reshape(64, 8, WIDE), BOTH, 0, 0, axis_index_groups=groups, tiled=True)
    return jnp.sum(parts, axis=0)


def body(entities, relations, src_index, dst_index, rel_index, neg_block):
    own = jnp.swapaxes(entities, 1, 2)
    target = lax.all_gather(own, "row", axis=0)
    rel = gather_rows([(jnp.swapaxes(relations, 1, 2), 0, None)], jnp.zeros((1,), jnp.int32), rel_index)
    pieces, order, rel = column_shards(own, rel)
    src = gather_rows(pieces, order, src_index)
    core = lax.axis_index("row") % 2
    places = (((rel_index >> 6) & 1) ^ core) * 512 + (rel_index >> 7) * 64 + (rel_index & 63)
    loss, keep, give = score_groups(target, dst_index, neg_block, src, rel, places)
    share = sum_at_owner(keep, give)
    share = jnp.stack([share[:, :DIM], share[:, HALF : HALF + DIM]])
    return loss.reshape(EDGES), share


def solution(mesh):
    placed = (
        P(None, BOTH, None),
        P(),
        P(BOTH),
        P(BOTH),
        P(BOTH),
        P(BOTH),
    )
    return jax.shard_map(
        body,
        mesh=mesh,
        in_specs=placed,
        out_specs=(P(BOTH), P(None, BOTH, None)),
        check_vma=False,
    )
```

```python
import functools

import jax
import jax.numpy as jnp
from jax import lax
from jax.experimental import pallas as pl
from jax.experimental.pallas import tpu as pltpu
from jax.sharding import PartitionSpec as P

F32, BF16 = jnp.float32, jnp.bfloat16
SHARD = 1024
EDGES = 4096
GROUP = 512
NEGB = 512
HALF = 256
WIDE = 2 * HALF
DIM = 200
NREL = 1024
STEPS = EDGES // GROUP
BOTH = ("row", "col")


def hop(array, dy=0, flip=0):
    pairs = []
    for r in range(16):
        for c in range(8):
            y, h = c // 2, c % 2
            pairs.append((r * 8 + c, r * 8 + ((y + dy) % 4) * 2 + (h ^ flip)))
    return lax.ppermute(array, BOTH, pairs)


def column_shards(own, first):
    tie = lax.optimization_barrier

    def ring(held, *rest):
        near = tie((hop(held, dy=1), hop(held, dy=-1), *rest))
        far = hop(near[0][:1], dy=1), hop(near[1][1:], dy=-1)
        return near, far

    pair = hop(own, flip=1)
    (*near, first), far = ring(own, first)
    pair, *far = tie((pair, *far))
    pair_near, pair_far = ring(pair)
    pieces = [(own, 0, None), (near[0], 1, None), (near[1], 2, None), (far[0], 3, 0), (far[1], 3, 1)]
    pieces += [(pair, 4, None), (pair_near[0], 5, None), (pair_near[1], 6, None), (pair_far[0], 7, 0), (pair_far[1], 7, 1)]
    c = lax.axis_index("col")
    y, h = c // 2, c % 2
    order = jnp.stack([((y + dy) % 4) * 2 + (h ^ flip) for flip in (0, 1) for dy in (0, -1, 1, 2)])
    return pieces, order.astype(jnp.int32), first


def fill_rows(columns, start, table):
    def tile(t, carry):
        n = pl.multiple_of(t * 128, 128)
        for part in range(2):
            head = columns[part, 0:128, pl.ds(n, 128)]
            tail = columns[part, 128:DIM, pl.ds(n, 128)].astype(F32)
            tail = jnp.concatenate([tail, jnp.zeros((HALF - DIM, 128), F32)], 0).astype(BF16)
            at = part * HALF
            table[pl.ds(start + n, 128), at : at + 128] = head.T.astype(F32)
            table[pl.ds(start + n, 128), at + 128 : at + HALF] = tail.T.astype(F32)
        return carry

    lax.fori_loop(0, SHARD // 128, tile, 0, unroll=8)


def pick_rows(index, first, table, rows, unroll=16):
    def step(i, carry):
        b = i * unroll
        values = [table[pl.ds(index[first + b + u], 1), :] for u in range(unroll)]
        for u in range(0, unroll, 8):
            rows[pl.ds(pl.multiple_of(b + u, 8), 8), :] = jnp.concatenate(values[u : u + 8], 0)
        return carry

    lax.fori_loop(0, GROUP // unroll, step, 0)


def gather_kernel(places, index, order, *refs):
    count = len(places)
    pieces, out = refs[:count], refs[count]
    held, table, rows, sem = refs[count + 1 :]
    g = pl.program_id(0)

    @pl.when(g == 0)
    def _():
        copies = []
        for piece, (slot, part) in zip(pieces, places):
            into = held.at[slot] if part is None else held.at[slot, pl.ds(part, 1)]
            copies.append(pltpu.make_async_copy(piece, into, sem.at[len(copies)]))
            copies[-1].start()
        for j, (slot, part) in enumerate(places):
            copies[j].wait()
            if part != 0:
                fill_rows(held.at[slot], pl.multiple_of(order[slot] * SHARD, SHARD), table)

    pick_rows(index, g * GROUP, table, rows)
    out[...] = rows[...].astype(BF16)


def gather_rows(pieces, order, index):
    places = tuple((slot, part) for _, slot, part in pieces)
    count = places[-1][0] + 1
    return pl.pallas_call(
        functools.partial(gather_kernel, places),
        out_shape=jax.ShapeDtypeStruct((EDGES, WIDE), BF16),
        grid_spec=pltpu.PrefetchScalarGridSpec(
            num_scalar_prefetch=2,
            grid=(STEPS,),
            in_specs=[pl.BlockSpec(memory_space=pl.ANY)] * len(places),
            out_specs=pl.BlockSpec((GROUP, WIDE), lambda g, *_: (g, 0)),
            scratch_shapes=[
                pltpu.VMEM((count, 2, DIM, SHARD), BF16),
                pltpu.VMEM((count * SHARD, WIDE), F32),
                pltpu.VMEM((GROUP, WIDE), F32),
                pltpu.SemaphoreType.DMA((len(places),)),
            ],
        ),
        compiler_params=pltpu.CompilerParams(vmem_limit_bytes=60 << 20),
        cost_estimate=pl.CostEstimate(flops=0, bytes_accessed=(5 + 2 * count) * 4_000_000, transcendentals=0),
        name="gather_rows",
    )(index, order, *[piece for piece, _, _ in pieces])


AHEAD = 6
BLOCK = 256
CHUNK = 16


def group_kernel(index, blocks, target, src, rel, rel_ids, loss, keep, give, held, table, rows, negs, terms, query, wide, pull, losses, sem):
    g = pl.program_id(0)

    @pl.when(g == 0)
    def _():
        copies = [pltpu.make_async_copy(target.at[j], held.at[j], sem.at[j]) for j in range(16)]
        for copy in copies[:AHEAD]:
            copy.start()
        negs[...] = jnp.zeros_like(negs)
        keep[...] = jnp.zeros_like(keep)
        give[...] = jnp.zeros_like(give)
        for j in range(16):
            copies[j].wait()
            if j + AHEAD < 16:
                copies[j + AHEAD].start()
            fill_rows(held.at[j], j * SHARD, table)

    @pl.when(g == 0)
    def _():
        pick_rows(index, 0, table, rows)
    block = blocks[g]
    half = pl.multiple_of((block % 2) * NEGB, NEGB)
    for part in range(2):
        negs[part * HALF : part * HALF + DIM, :] = held[block // 2, part, :, pl.ds(half, NEGB)]

    nxt = jnp.minimum(g + 1, STEPS - 1) * GROUP
    tiles = [slice(k * 128, (k + 1) * 128) for k in range(4)]

    def queries(at):
        s = [src[at, t].astype(F32) for t in tiles]
        w = [rel[at, t].astype(F32) for t in tiles]
        o = [rows[at, t] for t in tiles]
        q = [s[0] * w[0] - s[2] * w[2], s[1] * w[1] - s[3] * w[3], s[0] * w[2] + s[2] * w[0], s[1] * w[3] + s[3] * w[1]]
        pos = jnp.sum((q[0] * o[0] + q[1] * o[1]) + (q[2] * o[2] + q[3] * o[3]), axis=1, keepdims=True)
        for t, v in zip(tiles, q):
            query[at, t] = v.astype(BF16)
        low = jnp.exp(-jnp.abs(pos))
        pull[at, :] = jnp.broadcast_to(jnp.where(pos >= 0, low, 1.0) / (1.0 + low), (CHUNK, 128))
        losses[at, :] = jnp.broadcast_to((jnp.maximum(-pos, 0.0) + jnp.log1p(low)) * (1.0 / 128), (CHUNK, 128))

    def weights(at):
        for k, t in enumerate(tiles):
            score = wide[at, t]
            low = jnp.exp(-jnp.abs(score))
            up = 1.0 + low
            query[at, t] = (jnp.where(score >= 0, 1.0 / NEGB, low * (1.0 / NEGB)) / up).astype(BF16)
            peak = jnp.maximum(score, 0.0)
            excess = excess * up + low if k else low
            total = total + peak if k else peak
        losses[at, :] += (total + jnp.log1p(excess)) * (1.0 / NEGB)

    def gradients(at):
        s = [src[at, t].astype(F32) for t in tiles]
        p = pull[at, :]
        d = [wide[at, t] - p * rows[at, t] for t in tiles]
        term = [d[0] * s[0] + d[2] * s[2], d[1] * s[1] + d[3] * s[3], d[2] * s[0] - d[0] * s[2], d[3] * s[1] - d[1] * s[3]]
        for t, v in zip(tiles, term):
            terms[at, t] = v.astype(BF16)
        for b in range(at.start, at.stop, 8):
            rows[b : b + 8, :] = jnp.concatenate([table[pl.ds(index[nxt + b + u], 1), :] for u in range(8)], 0)

    blocks_of = [slice(b, b + BLOCK) for b in range(0, GROUP, BLOCK)]
    chunks_of = lambda block: [slice(c, c + CHUNK) for c in range(block.start, block.stop, CHUNK)]
    for block in blocks_of:
        for at in chunks_of(block):
            queries(at)
        wide[block, :] = jnp.dot(query[block, :], negs[...], preferred_element_type=F32)
    for block in blocks_of:
        for at in chunks_of(block):
            weights(at)
        wide[block, :] = lax.dot_general(query[block, :], negs[...], (((1,), (1,)), ((), ())), preferred_element_type=F32)
    for block in blocks_of:
        for at in chunks_of(block):
            gradients(at)
    for b in range(0, GROUP, 128):
        loss[0, :, b : b + 128] = jnp.sum(losses[b : b + 128, :].T, axis=0, keepdims=True)
    ids = rel_ids[0]

    hot = lax.broadcasted_iota(jnp.int32, (NREL, GROUP), 0) == ids
    hot = jnp.where(hot, 1.0, 0.0).astype(BF16)
    grad = jnp.dot(hot, terms[...], preferred_element_type=F32)
    keep[...] += grad[: NREL // 2]
    give[...] += grad[NREL // 2 :]


def score_groups(target, dst_index, neg_block, src, rel, places):
    return pl.pallas_call(
        group_kernel,
        out_shape=(
            jax.ShapeDtypeStruct((STEPS, 1, GROUP), F32),
            jax.ShapeDtypeStruct((NREL // 2, WIDE), F32),
            jax.ShapeDtypeStruct((NREL // 2, WIDE), F32),
        ),
        grid_spec=pltpu.PrefetchScalarGridSpec(
            num_scalar_prefetch=2,
            grid=(STEPS,),
            in_specs=[
                pl.BlockSpec(memory_space=pl.ANY),
                pl.BlockSpec((GROUP, WIDE), lambda g, *_: (g, 0)),
                pl.BlockSpec((GROUP, WIDE), lambda g, *_: (g, 0)),
                pl.BlockSpec((1, 1, GROUP), lambda g, *_: (g, 0, 0)),
            ],
            out_specs=[
                pl.BlockSpec((1, 1, GROUP), lambda g, *_: (g, 0, 0)),
                pl.BlockSpec((NREL // 2, WIDE), lambda g, *_: (0, 0)),
                pl.BlockSpec((NREL // 2, WIDE), lambda g, *_: (0, 0)),
            ],
            scratch_shapes=[
                pltpu.VMEM((16, 2, DIM, SHARD), BF16),
                pltpu.VMEM((16 * SHARD, WIDE), F32),
                pltpu.VMEM((GROUP, WIDE), F32),
                pltpu.VMEM((WIDE, NEGB), BF16),
                pltpu.VMEM((GROUP, WIDE), BF16),
                pltpu.VMEM((GROUP, WIDE), BF16),
                pltpu.VMEM((GROUP, WIDE), F32),
                pltpu.VMEM((GROUP, 128), F32),
                pltpu.VMEM((GROUP, 128), F32),
                pltpu.SemaphoreType.DMA((16,)),
            ],
        ),
        compiler_params=pltpu.CompilerParams(vmem_limit_bytes=60 << 20),
        cost_estimate=pl.CostEstimate(flops=20_000_000_000, bytes_accessed=24_000_000, transcendentals=4_000_000),
        name="score_groups",
    )(dst_index, neg_block, target, src, rel, places.reshape(STEPS, 1, GROUP))


def sum_at_owner(keep, give):
    half = keep + lax.ppermute(give, BOTH, [(d, d ^ 8) for d in range(128)])
    groups = [[a * 16 + core * 8 + c for a in range(8) for c in range(8)] for core in range(2)]
    parts = lax.all_to_all(half.reshape(64, 8, WIDE), BOTH, 0, 0, axis_index_groups=groups, tiled=True)
    return jnp.sum(parts, axis=0)


def body(entities, relations, src_index, dst_index, rel_index, neg_block):
    own = jnp.swapaxes(entities, 1, 2)
    target = lax.all_gather(own, "row", axis=0)
    rel = gather_rows([(jnp.swapaxes(relations, 1, 2), 0, None)], jnp.zeros((1,), jnp.int32), rel_index)
    pieces, order, rel = column_shards(own, rel)
    src = gather_rows(pieces, order, src_index)
    core = lax.axis_index("row") % 2
    places = (((rel_index >> 6) & 1) ^ core) * 512 + (rel_index >> 7) * 64 + (rel_index & 63)
    loss, keep, give = score_groups(target, dst_index, neg_block, src, rel, places)
    share = sum_at_owner(keep, give)
    share = jnp.stack([share[:, :DIM], share[:, HALF : HALF + DIM]])
    return loss.reshape(EDGES), share


def solution(mesh):
    placed = (
        P(None, BOTH, None),
        P(),
        P(BOTH),
        P(BOTH),
        P(BOTH),
        P(BOTH),
    )
    return jax.shard_map(
        body,
        mesh=mesh,
        in_specs=placed,
        out_specs=(P(BOTH), P(None, BOTH, None)),
        check_vma=False,
    )
```

```python
import functools

import jax
import jax.numpy as jnp
from jax import lax
from jax.experimental import pallas as pl
from jax.experimental.pallas import tpu as pltpu
from jax.sharding import PartitionSpec as P

F32, BF16 = jnp.float32, jnp.bfloat16
SHARD = 1024
EDGES = 4096
GROUP = 512
NEGB = 512
HALF = 256
WIDE = 2 * HALF
DIM = 200
NREL = 1024
STEPS = EDGES // GROUP
BOTH = ("row", "col")


def hop(array, dy=0, flip=0):
    pairs = []
    for r in range(16):
        for c in range(8):
            y, h = c // 2, c % 2
            pairs.append((r * 8 + c, r * 8 + ((y + dy) % 4) * 2 + (h ^ flip)))
    return lax.ppermute(array, BOTH, pairs)


def column_shards(own, first):
    tie = lax.optimization_barrier

    def ring(held, *rest):
        near = tie((hop(held, dy=1), hop(held, dy=-1), *rest))
        far = hop(near[0][:1], dy=1), hop(near[1][1:], dy=-1)
        return near, far

    pair = hop(own, flip=1)
    (*near, first), far = ring(own, first)
    pair, *far = tie((pair, *far))
    pair_near, pair_far = ring(pair)
    pieces = [(own, 0, None), (near[0], 1, None), (near[1], 2, None), (far[0], 3, 0), (far[1], 3, 1)]
    pieces += [(pair, 4, None), (pair_near[0], 5, None), (pair_near[1], 6, None), (pair_far[0], 7, 0), (pair_far[1], 7, 1)]
    c = lax.axis_index("col")
    y, h = c // 2, c % 2
    order = jnp.stack([((y + dy) % 4) * 2 + (h ^ flip) for flip in (0, 1) for dy in (0, -1, 1, 2)])
    return pieces, order.astype(jnp.int32), first


def fill_rows(columns, start, table):
    def tile(t, carry):
        n = pl.multiple_of(t * 128, 128)
        for part in range(2):
            head = columns[part, 0:128, pl.ds(n, 128)]
            tail = columns[part, 128:DIM, pl.ds(n, 128)].astype(F32)
            tail = jnp.concatenate([tail, jnp.zeros((HALF - DIM, 128), F32)], 0).astype(BF16)
            at = part * HALF
            table[pl.ds(start + n, 128), at : at + 128] = head.T.astype(F32)
            table[pl.ds(start + n, 128), at + 128 : at + HALF] = tail.T.astype(F32)
        return carry

    lax.fori_loop(0, SHARD // 128, tile, 0, unroll=8)


def pick_rows(index, first, table, rows, unroll=64):
    def step(i, carry):
        b = i * unroll
        values = [table[pl.ds(index[first + b + u], 1), :] for u in range(unroll)]
        for u in range(0, unroll, 8):
            rows[pl.ds(pl.multiple_of(b + u, 8), 8), :] = jnp.concatenate(values[u : u + 8], 0)
        return carry

    lax.fori_loop(0, GROUP // unroll, step, 0)


def gather_kernel(places, index, order, *refs):
    count = len(places)
    pieces, out = refs[:count], refs[count]
    held, table, rows, sem = refs[count + 1 :]
    g = pl.program_id(0)

    @pl.when(g == 0)
    def _():
        copies = []
        for piece, (slot, part) in zip(pieces, places):
            into = held.at[slot] if part is None else held.at[slot, pl.ds(part, 1)]
            copies.append(pltpu.make_async_copy(piece, into, sem.at[len(copies)]))
            copies[-1].start()
        for j, (slot, part) in enumerate(places):
            copies[j].wait()
            if part != 0:
                fill_rows(held.at[slot], pl.multiple_of(order[slot] * SHARD, SHARD), table)

    pick_rows(index, g * GROUP, table, rows)
    out[...] = rows[...].astype(BF16)


def gather_rows(pieces, order, index):
    places = tuple((slot, part) for _, slot, part in pieces)
    count = places[-1][0] + 1
    return pl.pallas_call(
        functools.partial(gather_kernel, places),
        out_shape=jax.ShapeDtypeStruct((EDGES, WIDE), BF16),
        grid_spec=pltpu.PrefetchScalarGridSpec(
            num_scalar_prefetch=2,
            grid=(STEPS,),
            in_specs=[pl.BlockSpec(memory_space=pl.ANY)] * len(places),
            out_specs=pl.BlockSpec((GROUP, WIDE), lambda g, *_: (g, 0)),
            scratch_shapes=[
                pltpu.VMEM((count, 2, DIM, SHARD), BF16),
                pltpu.VMEM((count * SHARD, WIDE), F32),
                pltpu.VMEM((GROUP, WIDE), F32),
                pltpu.SemaphoreType.DMA((len(places),)),
            ],
        ),
        compiler_params=pltpu.CompilerParams(vmem_limit_bytes=60 << 20),
        cost_estimate=pl.CostEstimate(flops=0, bytes_accessed=(5 + 2 * count) * 4_000_000, transcendentals=0),
        name="gather_rows",
    )(index, order, *[piece for piece, _, _ in pieces])


AHEAD = 16
BLOCK = 256
CHUNK = 16


def group_kernel(index, blocks, target, src, rel, rel_ids, loss, keep, give, held, table, rows, negs, terms, query, wide, pull, losses, sem):
    g = pl.program_id(0)

    @pl.when(g == 0)
    def _():
        copies = [pltpu.make_async_copy(target.at[j], held.at[j], sem.at[j]) for j in range(16)]
        for copy in copies[:AHEAD]:
            copy.start()
        negs[...] = jnp.zeros_like(negs)
        keep[...] = jnp.zeros_like(keep)
        give[...] = jnp.zeros_like(give)
        for j in range(16):
            copies[j].wait()
            if j + AHEAD < 16:
                copies[j + AHEAD].start()
            fill_rows(held.at[j], j * SHARD, table)

    @pl.when(g == 0)
    def _():
        pick_rows(index, 0, table, rows)
    block = blocks[g]
    half = pl.multiple_of((block % 2) * NEGB, NEGB)
    for part in range(2):
        negs[part * HALF : part * HALF + DIM, :] = held[block // 2, part, :, pl.ds(half, NEGB)]

    nxt = jnp.minimum(g + 1, STEPS - 1) * GROUP
    tiles = [slice(k * 128, (k + 1) * 128) for k in range(4)]

    def queries(at):
        s = [src[at, t].astype(F32) for t in tiles]
        w = [rel[at, t].astype(F32) for t in tiles]
        o = [rows[at, t] for t in tiles]
        q = [s[0] * w[0] - s[2] * w[2], s[1] * w[1] - s[3] * w[3], s[0] * w[2] + s[2] * w[0], s[1] * w[3] + s[3] * w[1]]
        pos = jnp.sum((q[0] * o[0] + q[1] * o[1]) + (q[2] * o[2] + q[3] * o[3]), axis=1, keepdims=True)
        for t, v in zip(tiles, q):
            query[at, t] = v.astype(BF16)
        low = jnp.exp(-jnp.abs(pos))
        pull[at, :] = jnp.broadcast_to(jnp.where(pos >= 0, low, 1.0) / (1.0 + low), (CHUNK, 128))
        losses[at, :] = jnp.broadcast_to((jnp.maximum(-pos, 0.0) + jnp.log1p(low)) * (1.0 / 128), (CHUNK, 128))

    def weights(at):
        for k, t in enumerate(tiles):
            score = wide[at, t]
            low = jnp.exp(-jnp.abs(score))
            up = 1.0 + low
            query[at, t] = (jnp.where(score >= 0, 1.0 / NEGB, low * (1.0 / NEGB)) / up).astype(BF16)
            peak = jnp.maximum(score, 0.0)
            excess = excess * up + low if k else low
            total = total + peak if k else peak
        losses[at, :] += (total + jnp.log1p(excess)) * (1.0 / NEGB)

    def gradients(at):
        s = [src[at, t].astype(F32) for t in tiles]
        p = pull[at, :]
        d = [wide[at, t] - p * rows[at, t] for t in tiles]
        term = [d[0] * s[0] + d[2] * s[2], d[1] * s[1] + d[3] * s[3], d[2] * s[0] - d[0] * s[2], d[3] * s[1] - d[1] * s[3]]
        for t, v in zip(tiles, term):
            terms[at, t] = v.astype(BF16)
        for b in range(at.start, at.stop, 8):
            rows[b : b + 8, :] = jnp.concatenate([table[pl.ds(index[nxt + b + u], 1), :] for u in range(8)], 0)

    blocks_of = [slice(b, b + BLOCK) for b in range(0, GROUP, BLOCK)]
    chunks_of = lambda block: [slice(c, c + CHUNK) for c in range(block.start, block.stop, CHUNK)]
    for block in blocks_of:
        for at in chunks_of(block):
            queries(at)
        wide[block, :] = jnp.dot(query[block, :], negs[...], preferred_element_type=F32)
    for block in blocks_of:
        for at in chunks_of(block):
            weights(at)
        wide[block, :] = lax.dot_general(query[block, :], negs[...], (((1,), (1,)), ((), ())), preferred_element_type=F32)
    for block in blocks_of:
        for at in chunks_of(block):
            gradients(at)
    for b in range(0, GROUP, 128):
        loss[0, :, b : b + 128] = jnp.sum(losses[b : b + 128, :].T, axis=0, keepdims=True)
    ids = rel_ids[0]

    hot = lax.broadcasted_iota(jnp.int32, (NREL, GROUP), 0) == ids
    hot = jnp.where(hot, 1.0, 0.0).astype(BF16)
    grad = jnp.dot(hot, terms[...], preferred_element_type=F32)
    keep[...] += grad[: NREL // 2]
    give[...] += grad[NREL // 2 :]


def score_groups(target, dst_index, neg_block, src, rel, places):
    return pl.pallas_call(
        group_kernel,
        out_shape=(
            jax.ShapeDtypeStruct((STEPS, 1, GROUP), F32),
            jax.ShapeDtypeStruct((NREL // 2, WIDE), F32),
            jax.ShapeDtypeStruct((NREL // 2, WIDE), F32),
        ),
        grid_spec=pltpu.PrefetchScalarGridSpec(
            num_scalar_prefetch=2,
            grid=(STEPS,),
            in_specs=[
                pl.BlockSpec(memory_space=pl.ANY),
                pl.BlockSpec((GROUP, WIDE), lambda g, *_: (g, 0)),
                pl.BlockSpec((GROUP, WIDE), lambda g, *_: (g, 0)),
                pl.BlockSpec((1, 1, GROUP), lambda g, *_: (g, 0, 0)),
            ],
            out_specs=[
                pl.BlockSpec((1, 1, GROUP), lambda g, *_: (g, 0, 0)),
                pl.BlockSpec((NREL // 2, WIDE), lambda g, *_: (0, 0)),
                pl.BlockSpec((NREL // 2, WIDE), lambda g, *_: (0, 0)),
            ],
            scratch_shapes=[
                pltpu.VMEM((16, 2, DIM, SHARD), BF16),
                pltpu.VMEM((16 * SHARD, WIDE), F32),
                pltpu.VMEM((GROUP, WIDE), F32),
                pltpu.VMEM((WIDE, NEGB), BF16),
                pltpu.VMEM((GROUP, WIDE), BF16),
                pltpu.VMEM((GROUP, WIDE), BF16),
                pltpu.VMEM((GROUP, WIDE), F32),
                pltpu.VMEM((GROUP, 128), F32),
                pltpu.VMEM((GROUP, 128), F32),
                pltpu.SemaphoreType.DMA((16,)),
            ],
        ),
        compiler_params=pltpu.CompilerParams(vmem_limit_bytes=60 << 20),
        cost_estimate=pl.CostEstimate(flops=20_000_000_000, bytes_accessed=24_000_000, transcendentals=4_000_000),
        name="score_groups",
    )(dst_index, neg_block, target, src, rel, places.reshape(STEPS, 1, GROUP))


def sum_at_owner(keep, give):
    half = keep + lax.ppermute(give, BOTH, [(d, d ^ 8) for d in range(128)])
    groups = [[a * 16 + core * 8 + c for a in range(8) for c in range(8)] for core in range(2)]
    parts = lax.all_to_all(half.reshape(64, 8, WIDE), BOTH, 0, 0, axis_index_groups=groups, tiled=True)
    return jnp.sum(parts, axis=0)


def body(entities, relations, src_index, dst_index, rel_index, neg_block):
    own = jnp.swapaxes(entities, 1, 2)
    target = lax.all_gather(own, "row", axis=0)
    rel = gather_rows([(jnp.swapaxes(relations, 1, 2), 0, None)], jnp.zeros((1,), jnp.int32), rel_index)
    pieces, order, rel = column_shards(own, rel)
    src = gather_rows(pieces, order, src_index)
    core = lax.axis_index("row") % 2
    places = (((rel_index >> 6) & 1) ^ core) * 512 + (rel_index >> 7) * 64 + (rel_index & 63)
    loss, keep, give = score_groups(target, dst_index, neg_block, src, rel, places)
    share = sum_at_owner(keep, give)
    share = jnp.stack([share[:, :DIM], share[:, HALF : HALF + DIM]])
    return loss.reshape(EDGES), share


def solution(mesh):
    placed = (
        P(None, BOTH, None),
        P(),
        P(BOTH),
        P(BOTH),
        P(BOTH),
        P(BOTH),
    )
    return jax.shard_map(
        body,
        mesh=mesh,
        in_specs=placed,
        out_specs=(P(BOTH), P(None, BOTH, None)),
        check_vma=False,
    )
```
